32 devices in a mesh: dp: 2 (over y), expert: 16 (over z, x, core).
Axes of the slice: x: 2, y: 2, z: 4, core: 2. Of those that a mesh axis runs over, the one named last changes fastest.
Arguments:
- tokens: bfloat16 [4096, 2048], P(('dp', 'expert')), may hold values from -6 to 6
- grad_out: bfloat16 [4096, 2048], P(('dp', 'expert')), may hold values from -6 to 6
- expert_ids: int32 [4096, 8], P(('dp', 'expert')), may hold values from 0 to 15, all different within a row; in each aligned block of 128 rows (0 to 127, 128 to 255, ...) at most 72 rows name the same one
- route_weight: bfloat16 [4096, 8], P(('dp', 'expert')), may hold values from 0.049804688 to 1
- w_gate: bfloat16 [16, 2048, 384], P('expert', 'dp'), may hold values from -0.125 to 0.125
- w_up: bfloat16 [16, 2048, 384], P('expert', 'dp'), may hold values from -0.125 to 0.125
- w_down: bfloat16 [16, 384, 2048], P('expert', None, 'dp'), may hold values from -0.3125 to 0.3125
Outputs:
- grad_tokens: bfloat16 [4096, 2048], P(('dp', 'expert'))
- grad_route: bfloat16 [4096, 8], P(('dp', 'expert'))
The draws below stay inside these ranges and needn't reach their ends.
Inputs may be any that keep to these rules, and one draw needn't show every extreme that they name: `expert_ids`: each row names 8 different experts; among the 128 rows of one device no expert is named by more than 72 rows, and in every draw some expert is named by exactly 72 rows of some device.
All inputs are finite; a program needn't handle non-finite values.
Results may differ from the reference program's by a relative error of at most 0.012.
Values may be sent and summed in bfloat16 or wider, within the bound.
A program may use at most 128 MiB of HBM per device.

```python
import math
import jax
import jax.numpy as jnp
import numpy as np
from jax import lax

D = 2048
H = 384
TOPK = 8
TOK_DEV = 128
E = 16
CAP = 72
TOKENS = 4096


def block_scale(stream_key, shape, shards, smallest, top_value):
    def one(position, parts):
        steps = jax.random.uniform(jax.random.fold_in(jax.random.fold_in(stream_key, 6), position), (parts,), jnp.float32, smallest / len(shards), top_value / len(shards))
        return jnp.repeat(jnp.exp(steps), shape[position] // parts).reshape((-1,) + (1,) * (len(shape) - position - 1))

    loudness = one(*shards[0])
    for cut in shards[1:]:
        loudness = loudness * one(*cut)
    return loudness


def shared_out(key, own, number, rows, number_of, top, most, skew):
    sequence = jax.random.permutation(key, number_of)
    crowded, common = shares(number_of, rows * top, most, skew, True), shares(number_of, rows * top, most, skew, False)
    places = jnp.arange(number_of)

    def named(lengths, rotation):
        used = int((lengths > 0).sum())
        fixed = max(1, used // 4)
        passed = fixed + (places - fixed + rotation * (used - fixed)) % max(1, number_of - fixed)
        return jnp.zeros((number_of,), jnp.int32).at[sequence[jnp.where(places < fixed, places, passed)]].set(jnp.asarray(lengths, jnp.int32))

    lengths = jnp.where(number % 4 == 0, named(crowded, number // 4), named(common, number - number // 4 - 1))
    mixed = jax.random.permutation(jax.random.fold_in(own, 3), number_of)
    source_of, receiver = mixed[0:number_of // 2 * 2:2], mixed[1:number_of // 2 * 2:2]
    slack = jnp.minimum(lengths[source_of] - 1, most - lengths[receiver]) // 2
    slack = jnp.where((source_of == sequence[0]) | (receiver == sequence[0]) | (lengths[receiver] == 0), 0, jnp.maximum(slack, 0))
    passed = jax.random.randint(jax.random.fold_in(own, 4), (number_of // 2,), 0, 1 << 20) % (slack + 1)
    lengths = lengths.at[source_of].add(-passed).at[receiver].add(passed)
    members = jnp.searchsorted(jnp.cumsum(lengths), jnp.arange(rows * top), side="right").astype(jnp.int32)
    listing = members.reshape(top, rows).T
    listing = listing[jax.random.permutation(jax.random.fold_in(own, 1), rows)]
    rotation = jax.random.randint(jax.random.fold_in(own, 2), (rows, 1), 0, top)
    return jnp.take_along_axis(listing, (jnp.arange(top)[None, :] + rotation) % top, axis=1)


def shares(number_of, total, limit, skew, full):
    loads = [(1 << 20) // math.isqrt(grade ** skew) + 1 for grade in range(1, number_of + 1)]
    largest = limit if full else min(limit, max(-(-total // number_of), total * loads[0] // sum(loads)))
    least = 1 if total - largest >= number_of - 1 else 0
    given, spare = [largest] + [least] * (number_of - 1), total - largest - least * (number_of - 1)
    while spare > 0:
        movable = [i for i in range(1, number_of) if given[i] < largest] or [i for i in range(1, number_of) if given[i] < limit]
        mass, remaining = sum([loads[i] for i in movable]), spare
        for i in movable:
            extra = min(limit - given[i], max(1, remaining * loads[i] // mass), spare)
            given[i] = given[i] + extra
            spare = spare - extra
    return np.array(given)


def noise(key, dims, scale, reach, pieces=(), kind=jnp.bfloat16):
    array = jax.random.normal(key, dims, jnp.float32) * scale
    if len(pieces) > 0:
        array = block_scale(key, dims, pieces, -0.22, 0.18) * array
    return jnp.clip(array, min=-reach, max=reach).astype(kind)


def setup_inputs(seed: int = 0) -> dict:
    key_list = jax.random.split(jax.random.key(seed), 8)
    tokens = noise(key_list[0], (TOKENS, D), 1.0, 6.0, ((0, 32),))
    grad_out = noise(key_list[1], (TOKENS, D), 1.0, 6.0, ((0, 32),))
    expert_ids_keys = jax.random.split(jax.random.fold_in(key_list[2], 1), TOKENS // TOK_DEV)
    expert_ids_turns = jax.random.permutation(jax.random.fold_in(key_list[2], 3), TOKENS // TOK_DEV)
    expert_ids = jax.vmap(lambda own, number: shared_out(jax.random.fold_in(key_list[2], 2), own, number, TOK_DEV, E, TOPK, CAP, 2))(expert_ids_keys, expert_ids_turns).reshape((TOKENS, TOPK))
    route_weight = jnp.clip(jnp.exp(math.log(1.0) - 2.9996462 * jax.random.uniform(key_list[3], (TOKENS, TOPK), jnp.float32) ** block_scale(key_list[3], (TOKENS, TOPK), ((0, 32),), -0.2, 0.2)), 0.049804688, 1.0).astype(jnp.bfloat16)
    w_gate = noise(key_list[4], (E, D, H), D ** -0.5, 0.125, ((0, 16), (1, 2)))
    w_up = noise(key_list[5], (E, D, H), D ** -0.5, 0.125, ((0, 16), (1, 2)))
    w_down = noise(key_list[6], (E, H, D), H ** -0.5, 0.3125, ((0, 16), (2, 2)))
    return dict(tokens=tokens, grad_out=grad_out, expert_ids=expert_ids, route_weight=route_weight, w_gate=w_gate, w_up=w_up, w_down=w_down)


def expert_rows(x_rows, g_rows, weight_rows, gate_mat, up_mat, down_mat):
    gate_pre = jnp.dot(x_rows, gate_mat, preferred_element_type=jnp.float32)
    up_pre = jnp.dot(x_rows, up_mat, preferred_element_type=jnp.float32)
    sigmoid_gate = jax.nn.sigmoid(gate_pre)
    active = gate_pre * sigmoid_gate
    hidden = active * up_pre
    back_hidden = jnp.dot(g_rows, down_mat.T, preferred_element_type=jnp.float32)
    route_grad = jnp.sum(hidden * back_hidden, axis=1)
    scaled = weight_rows.astype(jnp.float32)[:, None] * back_hidden
    slope = sigmoid_gate * (1.0 + gate_pre * (1.0 - sigmoid_gate))
    d_gate = (scaled * up_pre * slope).astype(jnp.bfloat16)
    d_up = (scaled * active).astype(jnp.bfloat16)
    input_grad = jnp.dot(d_gate, gate_mat.T, preferred_element_type=jnp.float32) + jnp.dot(d_up, up_mat.T, preferred_element_type=jnp.float32)
    return input_grad.astype(jnp.bfloat16), route_grad.astype(jnp.bfloat16)


def reference(tokens, grad_out, expert_ids, route_weight, w_gate, w_up, w_down):
    tok_total = tokens.shape[0]
    top_k = expert_ids.shape[1]
    n_assign = tok_total * top_k
    n_experts = w_gate.shape[0]
    flat_ids = expert_ids.reshape(-1).astype(jnp.int32)
    flat_weight = route_weight.reshape(-1)
    sorted_order = jnp.argsort(flat_ids, stable=True).astype(jnp.int32)
    counts = jnp.zeros((n_experts,), jnp.int32).at[flat_ids].add(1)
    starts = (jnp.cumsum(counts) - counts).astype(jnp.int32)
    block_rows = 1024
    order_pad = jnp.concatenate([sorted_order, jnp.zeros((block_rows,), jnp.int32)])

    def per_expert(totals, inputs):
        gate_mat, up_mat, down_mat, expert_index = inputs

        def per_block(block_index, running):
            acc_grad, acc_route = running
            offset = (block_index * block_rows).astype(jnp.int32)
            picked = lax.dynamic_slice_in_dim(order_pad, (starts[expert_index] + offset).astype(jnp.int32), block_rows)
            is_live = offset + jnp.arange(block_rows, dtype=jnp.int32) < counts[expert_index]
            token_of = picked // top_k
            grad_rows, routes = expert_rows(tokens[token_of], grad_out[token_of], flat_weight[picked], gate_mat, up_mat, down_mat)
            acc_grad = acc_grad.at[jnp.where(is_live, token_of, tok_total)].add(grad_rows.astype(jnp.float32), mode="drop")
            acc_route = acc_route.at[jnp.where(is_live, picked, n_assign)].set(routes, mode="drop")
            return acc_grad, acc_route

        n_blocks = (counts[expert_index] + block_rows - 1) // block_rows
        return lax.fori_loop(0, n_blocks, per_block, totals), None

    initial = (jnp.zeros((tok_total, tokens.shape[1]), jnp.float32), jnp.zeros((n_assign,), jnp.bfloat16))
    (acc_grad, acc_route), _ = lax.scan(per_expert, initial, (w_gate, w_up, w_down, jnp.arange(n_experts, dtype=jnp.int32)))
    return acc_grad.astype(jnp.bfloat16), acc_route.reshape(tok_total, top_k)
```

```python
import jax
import jax.numpy as jnp
from jax import lax
from jax.sharding import PartitionSpec as P


def expert_rows(x_rows, g_rows, weight_rows, gate_mat, up_mat, down_mat):
    gate_pre = jnp.dot(x_rows, gate_mat, preferred_element_type=jnp.float32)
    up_pre = jnp.dot(x_rows, up_mat, preferred_element_type=jnp.float32)
    sigmoid_gate = jax.nn.sigmoid(gate_pre)
    active = gate_pre * sigmoid_gate
    hidden = active * up_pre
    back_hidden = jnp.dot(g_rows, down_mat.T, preferred_element_type=jnp.float32)
    route_grad = jnp.sum(hidden * back_hidden, axis=1)
    scaled = weight_rows.astype(jnp.float32)[:, None] * back_hidden
    slope = sigmoid_gate * (1.0 + gate_pre * (1.0 - sigmoid_gate))
    d_gate = (scaled * up_pre * slope).astype(jnp.bfloat16)
    d_up = (scaled * active).astype(jnp.bfloat16)
    input_grad = jnp.dot(d_gate, gate_mat.T, preferred_element_type=jnp.float32) + jnp.dot(
        d_up, up_mat.T, preferred_element_type=jnp.float32
    )
    return (input_grad.astype(jnp.bfloat16), route_grad.astype(jnp.bfloat16))


def per_device(tokens, grad_out, expert_ids, route_weight, w_gate, w_up, w_down):
    tok_rows, width_model = tokens.shape
    n_expert = lax.axis_size("expert")
    gate_mat, up_mat, down_mat = (
        lax.all_gather(w_gate[0], "dp", axis=0, tiled=True),
        lax.all_gather(w_up[0], "dp", axis=0, tiled=True),
        lax.all_gather(w_down[0], "dp", axis=1, tiled=True),
    )
    chosen = expert_ids[:, :, None] == jnp.arange(n_expert, dtype=jnp.int32)[None, None, :]
    dense_w = jnp.sum(
        jnp.where(chosen, route_weight[:, :, None].astype(jnp.float32), 0.0), axis=1
    ).astype(jnp.bfloat16)
    weight_rows = lax.all_to_all(dense_w.T, "expert", split_axis=0, concat_axis=0, tiled=True)
    all_x = lax.all_gather(tokens, "expert", axis=0, tiled=True)
    all_g = lax.all_gather(grad_out, "expert", axis=0, tiled=True)
    out_grad, out_route = expert_rows(all_x, all_g, weight_rows.reshape(-1), gate_mat, up_mat, down_mat)
    grad_tokens = lax.psum_scatter(out_grad, "expert", scatter_dimension=0, tiled=True)
    back_route = lax.all_to_all(
        out_route.reshape(n_expert, tok_rows), "expert", split_axis=0, concat_axis=0, tiled=True
    )
    grad_route = jnp.sum(
        jnp.where(chosen, back_route.T[:, None, :].astype(jnp.float32), 0.0), axis=2
    ).astype(jnp.bfloat16)
    return (grad_tokens, grad_route)


def solution(mesh):
    return jax.shard_map(
        per_device,
        mesh=mesh,
        in_specs=(
            P(("dp", "expert"), None),
            P(("dp", "expert"), None),
            P(("dp", "expert"), None),
            P(("dp", "expert"), None),
            P("expert", "dp", None),
            P("expert", "dp", None),
            P("expert", None, "dp"),
        ),
        out_specs=(P(("dp", "expert"), None), P(("dp", "expert"), None)),
        check_vma=False,
    )
```

```python
import functools

import jax
import jax.numpy as jnp
from jax import lax
from jax.experimental import pallas as pl
from jax.experimental.pallas import tpu as pltpu
from jax.sharding import PartitionSpec as P


def expert_rows(x_rows, g_rows, weight_rows, gate_mat, up_mat, down_mat):
    gate_pre = jnp.dot(x_rows, gate_mat, preferred_element_type=jnp.float32)
    up_pre = jnp.dot(x_rows, up_mat, preferred_element_type=jnp.float32)
    sigmoid_gate = jax.nn.sigmoid(gate_pre)
    active = gate_pre * sigmoid_gate
    hidden = active * up_pre
    back_hidden = jnp.dot(g_rows, down_mat.T, preferred_element_type=jnp.float32)
    route_grad = jnp.sum(hidden * back_hidden, axis=1)
    scaled = weight_rows.astype(jnp.float32)[:, None] * back_hidden
    slope = sigmoid_gate * (1.0 + gate_pre * (1.0 - sigmoid_gate))
    d_gate = (scaled * up_pre * slope).astype(jnp.bfloat16)
    d_up = (scaled * active).astype(jnp.bfloat16)
    input_grad = jnp.dot(d_gate, gate_mat.T, preferred_element_type=jnp.float32) + jnp.dot(
        d_up, up_mat.T, preferred_element_type=jnp.float32
    )
    return (input_grad.astype(jnp.bfloat16), route_grad.astype(jnp.bfloat16))


def fetch_rows(tokens, grad_out, flat_weight, assign_of, top_k):
    token_of = assign_of // top_k
    rows_x = jnp.take(tokens, token_of, axis=0, mode="fill", fill_value=0)
    rows_g = jnp.take(grad_out, token_of, axis=0, mode="fill", fill_value=0)
    rows_w = jnp.take(flat_weight, assign_of, axis=0, mode="fill", fill_value=0)
    return (rows_x, rows_g, rows_w)


def per_device_exchange(tokens, grad_out, expert_ids, route_weight, w_gate, w_up, w_down):
    tok_rows, width_model = tokens.shape
    top_k = expert_ids.shape[1]
    n_assign = tok_rows * top_k
    n_expert = lax.axis_size("expert")
    capacity = 9 * tok_rows * top_k // (8 * n_expert)
    slots_all = n_expert * capacity
    gate_mat, up_mat, down_mat = (
        lax.all_gather(w_gate[0], "dp", axis=0, tiled=True),
        lax.all_gather(w_up[0], "dp", axis=0, tiled=True),
        lax.all_gather(w_down[0], "dp", axis=1, tiled=True),
    )
    flat_ids = expert_ids.reshape(-1)
    flat_weight = route_weight.reshape(-1)
    onehot = (flat_ids[:, None] == jnp.arange(n_expert, dtype=jnp.int32)[None, :]).astype(jnp.int32)
    earlier = jnp.cumsum(onehot, axis=0) - onehot
    slot_of = jnp.sum(earlier * onehot, axis=1)
    placed = flat_ids * capacity + slot_of
    assign_index = jnp.arange(n_assign, dtype=jnp.int32)
    slot_assign = (
        jnp.full((slots_all,), n_assign, jnp.int32).at[placed].set(assign_index, mode="drop")
    )
    send_x, send_g, send_w = fetch_rows(tokens, grad_out, flat_weight, slot_assign, top_k)
    send_x = send_x.reshape(n_expert, capacity, width_model)
    send_g = send_g.reshape(n_expert, capacity, width_model)
    send_w = send_w.reshape(n_expert, capacity)
    got_x, got_g, got_w = (
        lax.all_to_all(send_x, "expert", split_axis=0, concat_axis=0, tiled=True),
        lax.all_to_all(send_g, "expert", split_axis=0, concat_axis=0, tiled=True),
        lax.all_to_all(send_w, "expert", split_axis=0, concat_axis=0, tiled=True),
    )
    out_grad, out_route = expert_rows(
        got_x.reshape(slots_all, width_model),
        got_g.reshape(slots_all, width_model),
        got_w.reshape(slots_all),
        gate_mat,
        up_mat,
        down_mat,
    )
    out_grad = out_grad.reshape(n_expert, capacity, width_model)
    out_route = out_route.reshape(n_expert, capacity)
    back_grad, back_route = (
        lax.all_to_all(out_grad, "expert", split_axis=0, concat_axis=0, tiled=True),
        lax.all_to_all(out_route, "expert", split_axis=0, concat_axis=0, tiled=True),
    )
    part_flat = back_grad.reshape(slots_all, width_model)[placed]
    route_flat = back_route.reshape(slots_all)[placed]
    part_rows = part_flat.reshape(tok_rows, top_k, width_model)
    grad_tokens = jnp.sum(part_rows.astype(jnp.float32), axis=1).astype(jnp.bfloat16)
    grad_route = route_flat.reshape(tok_rows, top_k)
    return (grad_tokens, grad_route)


LANES = 128
MESH = pl.DeviceIdType.MESH


def gather_kernel(
    n_rows, x_in, g_in, route_in, gate_in, up_in, down_in, out_ref, out_route,
    all_x, all_g, w_in, w_down, part, from_sib, from_row, from_below, from_above,
    pre, back, d_both,
    load_sem, weight_load, weight_send, weight_recv,
    recv, send_up, send_down, send_row, send_sib, send_extra,
    sib_send, sib_recv, row_send, row_recv, col_send, below_recv, above_recv,
):
    me = lax.axis_index("expert")
    y = lax.axis_index("dp")
    z, x, core = me // 4, (me // 2) % 2, me % 2
    top = n_rows - 1
    tok, width = x_in.shape
    hidden = gate_in.shape[1]
    shard = gate_in.shape[0]
    half = tok // 2

    sib = {"expert": me + 1 - 2 * core}
    across = {"expert": me + 2 - 4 * x}
    above = {"expert": me + 4}
    below = {"expert": me - 4}
    twin = {"dp": 1 - y}

    upper = z // 2
    near = z + upper * (top - 2 * z)

    def row_of(k):
        r = near if k == 0 else (1 - near if k == 1 else k)
        return r + upper * (top - 2 * r)

    def row_of_traced(k):
        early = 1 - jnp.minimum(k // 2, 1)
        r = early * (near + k * (1 - 2 * near)) + (1 - early) * k
        return r + upper * (top - 2 * r)

    def index(row, col, c):
        return (row * 2 + col) * 2 + c

    bufs = (all_x, all_g)

    def remote(src, dst, s, r, who):
        return pltpu.make_async_remote_copy(
            src_ref=src, dst_ref=dst, send_sem=s, recv_sem=r, device_id=who, device_id_type=MESH
        )

    def block(p, e, s, who):
        return remote(bufs[p].at[e], bufs[p].at[e], s, recv.at[p, e], who)

    def wait_block(p, e):
        pltpu.make_async_copy(bufs[p].at[e], bufs[p].at[e], recv.at[p, e]).wait()

    loads = [
        pltpu.make_async_copy(x_in, all_x.at[me], load_sem.at[0]),
        pltpu.make_async_copy(g_in, all_g.at[me, :, pl.ds(0, width)], load_sem.at[1]),
        pltpu.make_async_copy(route_in, all_g.at[me, :, pl.ds(width, LANES)], load_sem.at[2]),
    ]
    rows = pl.ds(pl.multiple_of(y * shard, shard), shard)
    homes = [
        w_in.at[rows, pl.ds(0, hidden)],
        w_in.at[rows, pl.ds(hidden, hidden)],
        w_down.at[:, rows],
    ]
    for cp in loads:
        cp.start()
    weight_loads = [
        pltpu.make_async_copy(src, dst, weight_load.at[i])
        for i, (src, dst) in enumerate(zip((gate_in, up_in, down_in), homes))
    ]
    for cp in weight_loads:
        cp.start()

    barrier = pltpu.get_barrier_semaphore()
    for who in (sib, across, twin):
        pl.semaphore_signal(barrier, inc=1, device_id=who, device_id_type=MESH)

    @pl.when(z > 0)
    def _():
        pl.semaphore_signal(barrier, inc=1, device_id=below, device_id_type=MESH)

    @pl.when(z < top)
    def _():
        pl.semaphore_signal(barrier, inc=1, device_id=above, device_id_type=MESH)

    pl.semaphore_wait(barrier, 3 + jnp.minimum(z, 1) + jnp.minimum(top - z, 1))

    for cp in loads:
        cp.wait()

    def up_copy(p, row):
        return block(p, index(row, x, core), send_up.at[p, row], above)

    def down_copy(p, row):
        return block(p, index(row, x, core), send_down.at[p, row], below)

    def row_copy(p, row):
        return block(p, index(row, x, core), send_row.at[p, row], across)

    def sib_copy(p, row, col):
        return block(p, index(row, col, core), send_sib.at[p, row * 2 + col], sib)

    def extra_copy(way, who):
        return block(1, index(z, 1 - x, core), send_extra.at[way], who)

    def by_row(p, k):
        return None if p == 0 or k == 0 or k == 3 else (near == k - 1)

    def row_forward(p, k, action):
        cond = by_row(p, k)
        if cond is None:
            action()
        else:
            pl.when(jnp.logical_not(cond))(action)

    for p in (0, 1):

        @pl.when(z < top)
        def _(p=p):
            up_copy(p, z).start()

        @pl.when(z > 0)
        def _(p=p):
            down_copy(p, z).start()

        row_copy(p, z).start()
        sib_copy(p, z, x).start()

    weight_copies = []
    for i, cp in enumerate(weight_loads):
        cp.wait()
        c = remote(homes[i], homes[i], weight_send.at[i], weight_recv.at[i], twin)
        c.start()
        weight_copies.append(c)

    def column_arrival(p, k):
        row = row_of(k)
        wait_block(p, index(row, x, core))

        @pl.when(jnp.logical_and(row < z, z < top))
        def _():
            up_copy(p, row).start()

        @pl.when(jnp.logical_and(row > z, z > 0))
        def _():
            down_copy(p, row).start()

        row_forward(p, k, lambda: row_copy(p, row).start())
        sib_copy(p, row, x).start()

    def row_arrival(p, k):
        row = row_of(k)
        wait_block(p, index(row, 1 - x, core))
        if p == 1 and k == 0:

            @pl.when(jnp.logical_and(z > 0, z < top))
            def _():
                extra_copy(0, below).start()
                extra_copy(1, above).start()

        sib_copy(p, row, 1 - x).start()

    for k in (1, 2):
        for p in (0, 1):
            column_arrival(p, k)
            row_arrival(p, k - 1)

    @pl.when(near == 1)
    def _():
        column_arrival(0, 3)
        column_arrival(1, 3)

    for c in weight_copies:
        c.wait_recv()

    lane = lax.broadcasted_iota(jnp.int32, (half, LANES), 1)

    def chip_of(i):
        side = i % 2
        return row_of_traced(i // 2) * 2 + x + side * (1 - 2 * x)

    def compute(i):
        q = chip_of(i)
        other = 2 * q + 1 - core
        wait_block(0, other)
        wait_block(1, other)
        pair = pl.ds(2 * q, 2)

        @pl.loop(0, 2 * hidden // 256)
        def _(j):
            cols = pl.ds(pl.multiple_of(j * 256, 256), 256)
            pre[:, cols] = jnp.dot(
                all_x[pair].reshape(2 * tok, width), w_in[:, cols], preferred_element_type=jnp.float32
            )

        back[...] = lax.dot_general(
            all_g[pair, :, pl.ds(0, width)].reshape(2 * tok, width), w_down[...],
            (((1,), (1,)), ((), ())), preferred_element_type=jnp.float32,
        )

        @pl.loop(0, 4)
        def _(r):
            rs = pl.ds(pl.multiple_of(r * half, half), half)
            e, off = 2 * q + r // 2, pl.ds(pl.multiple_of((r % 2) * half, half), half)
            gate_pre = pre[rs, pl.ds(0, hidden)]
            up_pre = pre[rs, pl.ds(hidden, hidden)]
            back_hidden = back[rs, :]
            sig = jax.nn.sigmoid(gate_pre)
            active = gate_pre * sig
            route_grad = jnp.sum(active * up_pre * back_hidden, axis=1, keepdims=True)
            weights = all_g[e, off, pl.ds(width, LANES)].astype(jnp.float32)
            weight = jnp.sum(jnp.where(lane == me, weights, 0.0), axis=1, keepdims=True)
            scaled = weight * back_hidden
            slope = sig * (1.0 + gate_pre * (1.0 - sig))
            d_both[rs, pl.ds(0, hidden)] = (scaled * up_pre * slope).astype(jnp.bfloat16)
            d_both[rs, pl.ds(hidden, hidden)] = (scaled * active).astype(jnp.bfloat16)
            part[e, off, pl.ds(width, LANES)] = jnp.where(lane == me, route_grad, 0.0).astype(jnp.bfloat16)

        @pl.loop(0, width // 256)
        def _(j):
            cols = pl.ds(pl.multiple_of(j * 256, 256), 256)
            res = lax.dot_general(
                d_both[...], w_in[cols, :], (((1,), (1,)), ((), ())), preferred_element_type=jnp.float32
            )
            part[pair, :, cols] = res.astype(jnp.bfloat16).reshape(2, tok, 256)

        to_sib(q).start()

    def to_sib(q):
        return remote(part.at[2 * q + 1 - core], from_sib.at[q], sib_send.at[q], sib_recv.at[q], sib)

    def add_into(dst, src):
        dst[...] = (dst[...].astype(jnp.float32) + src[...].astype(jnp.float32)).astype(jnp.bfloat16)

    def finish(i):
        q = chip_of(i)
        to_sib(q).wait_recv()
        add_into(part.at[2 * q + core], from_sib.at[q])

    @pl.loop(0, 2 * n_rows)
    def _(i):
        @pl.when(i == 4)
        def _():
            for p in (0, 1):

                @pl.when(near == 0)
                def _(p=p):
                    column_arrival(p, 3)

                row_arrival(p, 2)

        @pl.when(i == 2 * n_rows - 1)
        def _():
            row_arrival(0, 3)
            row_arrival(1, 3)

        compute(i)

        @pl.when(i > 0)
        def _():
            finish(i - 1)

    finish(2 * n_rows - 1)

    def halves(h):
        return pl.ds(pl.multiple_of(h * half, half), half)

    def row_sum(row, h):
        return remote(
            part.at[index(row, 1 - x, core), halves(h)], from_row.at[row, halves(h)],
            row_send.at[row, h], row_recv.at[row, h], across,
        )

    def col_up(row, h):
        return remote(
            part.at[index(row, x, core), halves(h)], from_below.at[row, halves(h)],
            col_send.at[row, h], below_recv.at[row, h], above,
        )

    def col_down(row, h):
        return remote(
            part.at[index(row, x, core), halves(h)], from_above.at[row, halves(h)],
            col_send.at[row, h], above_recv.at[row, h], below,
        )

    @pl.loop(0, 2 * n_rows)
    def _(i):
        row_sum(row_of_traced(top - i // 2), i % 2).start()

    @pl.loop(0, 2 * n_rows)
    def _(i):
        row, h = row_of_traced(top - i // 2), i % 2
        mine = part.at[index(row, x, core), halves(h)]
        row_sum(row, h).wait_recv()
        add_into(mine, from_row.at[row, halves(h)])

        @pl.when(jnp.logical_and(row >= z, z > 0))
        def _():
            col_up(row, h).wait_recv()
            add_into(mine, from_below.at[row, halves(h)])

        @pl.when(jnp.logical_and(row <= z, z < top))
        def _():
            col_down(row, h).wait_recv()
            add_into(mine, from_above.at[row, halves(h)])

        @pl.when(row > z)
        def _():
            col_up(row, h).start()

        @pl.when(row < z)
        def _():
            col_down(row, h).start()

    out_ref[...] = part[me, :, pl.ds(0, width)]
    out_route[...] = part[me, :, pl.ds(width, LANES)]

    for c in weight_copies:
        c.wait_send()
    for k in range(n_rows):
        row = row_of(k)
        for p in (0, 1):
            if k == 0:

                @pl.when(z < top)
                def _(p=p):
                    up_copy(p, z).wait_send()

                @pl.when(z > 0)
                def _(p=p):
                    down_copy(p, z).wait_send()
            else:

                @pl.when(jnp.logical_and(row < z, z < top))
                def _(p=p, row=row):
                    up_copy(p, row).wait_send()

                @pl.when(jnp.logical_and(row > z, z > 0))
                def _(p=p, row=row):
                    down_copy(p, row).wait_send()

            row_forward(p, k, lambda p=p, row=row: row_copy(p, row).wait_send())
            sib_copy(p, row, x).wait_send()
            sib_copy(p, row, 1 - x).wait_send()

    @pl.when(jnp.logical_and(z > 0, z < top))
    def _():
        extra_copy(0, below).wait_send()
        extra_copy(1, above).wait_send()

    @pl.loop(0, 2 * n_rows)
    def _(i):
        to_sib(i).wait_send()
        row, h = i // 2, i % 2
        row_sum(row, h).wait_send()

        @pl.when(row != z)
        def _():
            col_up(row, h).wait_send()


def per_device_gather(tokens, grad_out, expert_ids, route_weight, w_gate, w_up, w_down):
    tok, width = tokens.shape
    n_expert = lax.axis_size("expert")
    n_rows = n_expert // 4
    hidden = w_gate.shape[2]
    chosen = expert_ids[:, :, None] == jnp.arange(LANES, dtype=jnp.int32)[None, None, :]
    dense = jnp.sum(jnp.where(chosen, route_weight[:, :, None].astype(jnp.float32), 0.0), axis=1)
    wide = width + LANES
    bf16, dma = jnp.bfloat16, pltpu.SemaphoreType.DMA
    vmem = pltpu.VMEM
    out, routes = pl.pallas_call(
        functools.partial(gather_kernel, n_rows),
        out_shape=(
            jax.ShapeDtypeStruct((tok, width), bf16),
            jax.ShapeDtypeStruct((tok, LANES), bf16),
        ),
        in_specs=[pl.BlockSpec(memory_space=pl.ANY)] * 6,
        out_specs=(pl.BlockSpec(memory_space=pltpu.VMEM), pl.BlockSpec(memory_space=pltpu.VMEM)),
        scratch_shapes=[
            vmem((n_expert, tok, width), bf16),
            vmem((n_expert, tok, wide), bf16),
            vmem((width, 2 * hidden), bf16),
            vmem((hidden, width), bf16),
            vmem((n_expert, tok, wide), bf16),
            vmem((n_expert // 2, tok, wide), bf16),
            vmem((n_rows, tok, wide), bf16),
            vmem((n_rows, tok, wide), bf16),
            vmem((n_rows, tok, wide), bf16),
            vmem((2 * tok, 2 * hidden), jnp.float32),
            vmem((2 * tok, hidden), jnp.float32),
            vmem((2 * tok, 2 * hidden), bf16),
            dma((3,)), dma((3,)), dma((3,)), dma((3,)),
            dma((2, n_expert)), dma((2, n_rows)), dma((2, n_rows)), dma((2, n_rows)),
            dma((2, n_expert // 2)), dma((2,)),
            dma((n_expert // 2,)), dma((n_expert // 2,)),
            dma((n_rows, 2)), dma((n_rows, 2)), dma((n_rows, 2)), dma((n_rows, 2)), dma((n_rows, 2)),
        ],
        compiler_params=pltpu.CompilerParams(
            collective_id=0, has_side_effects=True, vmem_limit_bytes=60 * 1024 * 1024
        ),
    )(tokens, grad_out, dense.astype(bf16), w_gate[0], w_up[0], w_down[0])
    grad_route = jnp.sum(
        jnp.where(chosen, routes[:, None, :].astype(jnp.float32), 0.0), axis=2
    ).astype(bf16)
    return (out, grad_route)


def per_device(*args):
    n_expert, top_k = lax.axis_size("expert"), args[2].shape[1]
    grid_fits = lax.axis_size("dp") == 2 and n_expert // 4 == 4 and n_expert % 4 == 0
    if grid_fits and 2 * top_k >= n_expert:
        return per_device_gather(*args)
    return per_device_exchange(*args)


def solution(mesh):
    return jax.shard_map(
        per_device,
        mesh=mesh,
        in_specs=(
            P(("dp", "expert"), None),
            P(("dp", "expert"), None),
            P(("dp", "expert"), None),
            P(("dp", "expert"), None),
            P("expert", "dp", None),
            P("expert", "dp", None),
            P("expert", None, "dp"),
        ),
        out_specs=(P(("dp", "expert"), None), P(("dp", "expert"), None)),
        check_vma=False,
    )
```

```python
import functools

import jax
import jax.numpy as jnp
from jax import lax
from jax.experimental import pallas as pl
from jax.experimental.pallas import tpu as pltpu
from jax.sharding import PartitionSpec as P


def expert_rows(x_rows, g_rows, weight_rows, gate_mat, up_mat, down_mat):
    gate_pre = jnp.dot(x_rows, gate_mat, preferred_element_type=jnp.float32)
    up_pre = jnp.dot(x_rows, up_mat, preferred_element_type=jnp.float32)
    sigmoid_gate = jax.nn.sigmoid(gate_pre)
    active = gate_pre * sigmoid_gate
    hidden = active * up_pre
    back_hidden = jnp.dot(g_rows, down_mat.T, preferred_element_type=jnp.float32)
    route_grad = jnp.sum(hidden * back_hidden, axis=1)
    scaled = weight_rows.astype(jnp.float32)[:, None] * back_hidden
    slope = sigmoid_gate * (1.0 + gate_pre * (1.0 - sigmoid_gate))
    d_gate = (scaled * up_pre * slope).astype(jnp.bfloat16)
    d_up = (scaled * active).astype(jnp.bfloat16)
    input_grad = jnp.dot(d_gate, gate_mat.T, preferred_element_type=jnp.float32) + jnp.dot(
        d_up, up_mat.T, preferred_element_type=jnp.float32
    )
    return (input_grad.astype(jnp.bfloat16), route_grad.astype(jnp.bfloat16))


def fetch_rows(tokens, grad_out, flat_weight, assign_of, top_k):
    token_of = assign_of // top_k
    rows_x = jnp.take(tokens, token_of, axis=0, mode="fill", fill_value=0)
    rows_g = jnp.take(grad_out, token_of, axis=0, mode="fill", fill_value=0)
    rows_w = jnp.take(flat_weight, assign_of, axis=0, mode="fill", fill_value=0)
    return (rows_x, rows_g, rows_w)


def per_device_exchange(tokens, grad_out, expert_ids, route_weight, w_gate, w_up, w_down):
    tok_rows, width_model = tokens.shape
    top_k = expert_ids.shape[1]
    n_assign = tok_rows * top_k
    n_expert = lax.axis_size("expert")
    capacity = 9 * tok_rows * top_k // (8 * n_expert)
    slots_all = n_expert * capacity
    gate_mat, up_mat, down_mat = (
        lax.all_gather(w_gate[0], "dp", axis=0, tiled=True),
        lax.all_gather(w_up[0], "dp", axis=0, tiled=True),
        lax.all_gather(w_down[0], "dp", axis=1, tiled=True),
    )
    flat_ids = expert_ids.reshape(-1)
    flat_weight = route_weight.reshape(-1)
    onehot = (flat_ids[:, None] == jnp.arange(n_expert, dtype=jnp.int32)[None, :]).astype(jnp.int32)
    earlier = jnp.cumsum(onehot, axis=0) - onehot
    slot_of = jnp.sum(earlier * onehot, axis=1)
    placed = flat_ids * capacity + slot_of
    assign_index = jnp.arange(n_assign, dtype=jnp.int32)
    slot_assign = (
        jnp.full((slots_all,), n_assign, jnp.int32).at[placed].set(assign_index, mode="drop")
    )
    send_x, send_g, send_w = fetch_rows(tokens, grad_out, flat_weight, slot_assign, top_k)
    send_x = send_x.reshape(n_expert, capacity, width_model)
    send_g = send_g.reshape(n_expert, capacity, width_model)
    send_w = send_w.reshape(n_expert, capacity)
    got_x, got_g, got_w = (
        lax.all_to_all(send_x, "expert", split_axis=0, concat_axis=0, tiled=True),
        lax.all_to_all(send_g, "expert", split_axis=0, concat_axis=0, tiled=True),
        lax.all_to_all(send_w, "expert", split_axis=0, concat_axis=0, tiled=True),
    )
    out_grad, out_route = expert_rows(
        got_x.reshape(slots_all, width_model),
        got_g.reshape(slots_all, width_model),
        got_w.reshape(slots_all),
        gate_mat,
        up_mat,
        down_mat,
    )
    out_grad = out_grad.reshape(n_expert, capacity, width_model)
    out_route = out_route.reshape(n_expert, capacity)
    back_grad, back_route = (
        lax.all_to_all(out_grad, "expert", split_axis=0, concat_axis=0, tiled=True),
        lax.all_to_all(out_route, "expert", split_axis=0, concat_axis=0, tiled=True),
    )
    part_flat = back_grad.reshape(slots_all, width_model)[placed]
    route_flat = back_route.reshape(slots_all)[placed]
    part_rows = part_flat.reshape(tok_rows, top_k, width_model)
    grad_tokens = jnp.sum(part_rows.astype(jnp.float32), axis=1).astype(jnp.bfloat16)
    grad_route = route_flat.reshape(tok_rows, top_k)
    return (grad_tokens, grad_route)


LANES = 128
MESH = pl.DeviceIdType.MESH


def gather_kernel(
    n_rows, x_in, g_in, route_in, gate_in, up_in, down_in, out_ref, out_route,
    all_x, all_g, w_in, w_down, part, from_sib, from_row, from_below, from_above,
    pre, back, d_both,
    load_sem, weight_load, weight_send, weight_recv,
    recv, send_up, send_down, send_row, send_sib, send_extra,
    sib_send, sib_recv, row_send, row_recv, col_send, below_recv, above_recv,
):
    me = lax.axis_index("expert")
    y = lax.axis_index("dp")
    z, x, core = me // 4, (me // 2) % 2, me % 2
    top = n_rows - 1
    tok, width = x_in.shape
    hidden = gate_in.shape[1]
    shard = gate_in.shape[0]
    half = tok // 2

    sib = {"expert": me + 1 - 2 * core}
    across = {"expert": me + 2 - 4 * x}
    above = {"expert": me + 4}
    below = {"expert": me - 4}
    twin = {"dp": 1 - y}

    upper = z // 2
    near = z + upper * (top - 2 * z)

    def row_of(k):
        r = near if k == 0 else (1 - near if k == 1 else k)
        return r + upper * (top - 2 * r)

    def row_of_traced(k):
        early = 1 - jnp.minimum(k // 2, 1)
        r = early * (near + k * (1 - 2 * near)) + (1 - early) * k
        return r + upper * (top - 2 * r)

    def index(row, col, c):
        return (row * 2 + col) * 2 + c

    bufs = (all_x, all_g)

    def remote(src, dst, s, r, who):
        return pltpu.make_async_remote_copy(
            src_ref=src, dst_ref=dst, send_sem=s, recv_sem=r, device_id=who, device_id_type=MESH
        )

    def block(p, e, s, who):
        return remote(bufs[p].at[e], bufs[p].at[e], s, recv.at[p, e], who)

    def wait_block(p, e):
        pltpu.make_async_copy(bufs[p].at[e], bufs[p].at[e], recv.at[p, e]).wait()

    loads = [
        pltpu.make_async_copy(x_in, all_x.at[me], load_sem.at[0]),
        pltpu.make_async_copy(g_in, all_g.at[me, :, pl.ds(0, width)], load_sem.at[1]),
        pltpu.make_async_copy(route_in, all_g.at[me, :, pl.ds(width, LANES)], load_sem.at[2]),
    ]
    rows = pl.ds(pl.multiple_of(y * shard, shard), shard)
    homes = [
        w_in.at[rows, pl.ds(0, hidden)],
        w_in.at[rows, pl.ds(hidden, hidden)],
        w_down.at[:, rows],
    ]
    for cp in loads:
        cp.start()
    weight_loads = [
        pltpu.make_async_copy(src, dst, weight_load.at[i])
        for i, (src, dst) in enumerate(zip((gate_in, up_in, down_in), homes))
    ]
    for cp in weight_loads:
        cp.start()

    barrier = pltpu.get_barrier_semaphore()
    for who in (sib, across, twin):
        pl.semaphore_signal(barrier, inc=1, device_id=who, device_id_type=MESH)

    @pl.when(z > 0)
    def _():
        pl.semaphore_signal(barrier, inc=1, device_id=below, device_id_type=MESH)

    @pl.when(z < top)
    def _():
        pl.semaphore_signal(barrier, inc=1, device_id=above, device_id_type=MESH)

    pl.semaphore_wait(barrier, 3 + jnp.minimum(z, 1) + jnp.minimum(top - z, 1))

    for cp in loads:
        cp.wait()

    def up_copy(p, row):
        return block(p, index(row, x, core), send_up.at[p, row], above)

    def down_copy(p, row):
        return block(p, index(row, x, core), send_down.at[p, row], below)

    def row_copy(p, row):
        return block(p, index(row, x, core), send_row.at[p, row], across)

    def sib_copy(p, row, col):
        return block(p, index(row, col, core), send_sib.at[p, row * 2 + col], sib)

    def extra_copy(way, who):
        return block(1, index(z, 1 - x, core), send_extra.at[way], who)

    def by_row(p, k):
        return None if p == 0 or k == 0 or k == 3 else (near == k - 1)

    def row_forward(p, k, action):
        cond = by_row(p, k)
        if cond is None:
            action()
        else:
            pl.when(jnp.logical_not(cond))(action)

    for p in (0, 1):

        @pl.when(z < top)
        def _(p=p):
            up_copy(p, z).start()

        @pl.when(z > 0)
        def _(p=p):
            down_copy(p, z).start()

        row_copy(p, z).start()
        sib_copy(p, z, x).start()

    weight_copies = []
    for i, cp in enumerate(weight_loads):
        cp.wait()
        c = remote(homes[i], homes[i], weight_send.at[i], weight_recv.at[i], twin)
        c.start()
        weight_copies.append(c)

    def column_arrival(p, k):
        row = row_of(k)
        wait_block(p, index(row, x, core))

        @pl.when(jnp.logical_and(row < z, z < top))
        def _():
            up_copy(p, row).start()

        @pl.when(jnp.logical_and(row > z, z > 0))
        def _():
            down_copy(p, row).start()

        row_forward(p, k, lambda: row_copy(p, row).start())
        sib_copy(p, row, x).start()

    def row_arrival(p, k):
        row = row_of(k)
        wait_block(p, index(row, 1 - x, core))
        sib_copy(p, row, 1 - x).start()

    @pl.when(near == 0)
    def _():
        for k in (1, 2):
            column_arrival(0, k)
            row_arrival(0, k - 1)
            column_arrival(1, k)
            if k == 1:
                row_arrival(1, 0)

    @pl.when(near == 1)
    def _():
        for p in (0, 1):
            column_arrival(p, 1)
            column_arrival(p, 2)
            row_arrival(p, 0)
        column_arrival(0, 3)
        row_arrival(0, 1)
        column_arrival(1, 3)
        extra_copy(0, below).start()
        extra_copy(1, above).start()
        row_arrival(1, 1)

    for c in weight_copies:
        c.wait_recv()

    lane = lax.broadcasted_iota(jnp.int32, (half, LANES), 1)

    def chip_of(i):
        last = i // (2 * n_rows - 1)
        outer = i + jnp.minimum(i // 3, 1) - 5 * last
        at_five, at_six = jnp.minimum(i // 5, 1), jnp.minimum(i // 6, 1)
        inner = i + at_five - 2 * at_six + last
        turn = outer + near * (inner - outer)
        side = turn % 2
        return row_of_traced(turn // 2) * 2 + x + side * (1 - 2 * x)

    def compute(i):
        q = chip_of(i)
        other = 2 * q + 1 - core
        wait_block(0, other)
        wait_block(1, other)
        pair = pl.ds(2 * q, 2)

        @pl.loop(0, 2 * hidden // 256)
        def _(j):
            cols = pl.ds(pl.multiple_of(j * 256, 256), 256)
            pre[:, cols] = jnp.dot(
                all_x[pair].reshape(2 * tok, width), w_in[:, cols], preferred_element_type=jnp.float32
            )

        back[...] = lax.dot_general(
            all_g[pair, :, pl.ds(0, width)].reshape(2 * tok, width), w_down[...],
            (((1,), (1,)), ((), ())), preferred_element_type=jnp.float32,
        )

        @pl.loop(0, 4)
        def _(r):
            rs = pl.ds(pl.multiple_of(r * half, half), half)
            e, off = 2 * q + r // 2, pl.ds(pl.multiple_of((r % 2) * half, half), half)
            gate_pre = pre[rs, pl.ds(0, hidden)]
            up_pre = pre[rs, pl.ds(hidden, hidden)]
            back_hidden = back[rs, :]
            sig = jax.nn.sigmoid(gate_pre)
            active = gate_pre * sig
            route_grad = jnp.sum(active * up_pre * back_hidden, axis=1, keepdims=True)
            weights = all_g[e, off, pl.ds(width, LANES)].astype(jnp.float32)
            weight = jnp.sum(jnp.where(lane == me, weights, 0.0), axis=1, keepdims=True)
            scaled = weight * back_hidden
            slope = sig * (1.0 + gate_pre * (1.0 - sig))
            d_both[rs, pl.ds(0, hidden)] = (scaled * up_pre * slope).astype(jnp.bfloat16)
            d_both[rs, pl.ds(hidden, hidden)] = (scaled * active).astype(jnp.bfloat16)
            part[e, off, pl.ds(width, LANES)] = jnp.where(lane == me, route_grad, 0.0).astype(jnp.bfloat16)

        @pl.loop(0, width // 256)
        def _(j):
            cols = pl.ds(pl.multiple_of(j * 256, 256), 256)
            res = lax.dot_general(
                d_both[...], w_in[cols, :], (((1,), (1,)), ((), ())), preferred_element_type=jnp.float32
            )
            part[pair, :, cols] = res.astype(jnp.bfloat16).reshape(2, tok, 256)

        to_sib(q).start()

    def to_sib(q):
        return remote(part.at[2 * q + 1 - core], from_sib.at[q], sib_send.at[q], sib_recv.at[q], sib)

    def add_into(dst, src):
        dst[...] = (dst[...].astype(jnp.float32) + src[...].astype(jnp.float32)).astype(jnp.bfloat16)

    def finish(i):
        q = chip_of(i)
        to_sib(q).wait_recv()
        add_into(part.at[2 * q + core], from_sib.at[q])

    def halves(h):
        return pl.ds(pl.multiple_of(h * half, half), half)

    def row_sum(row, h):
        return remote(
            part.at[index(row, 1 - x, core), halves(h)], from_row.at[row, halves(h)],
            row_send.at[row, h], row_recv.at[row, h], across,
        )

    def col_up(row, h):
        return remote(
            part.at[index(row, x, core), halves(h)], from_below.at[row, halves(h)],
            col_send.at[row, h], below_recv.at[row, h], above,
        )

    def col_down(row, h):
        return remote(
            part.at[index(row, x, core), halves(h)], from_above.at[row, halves(h)],
            col_send.at[row, h], above_recv.at[row, h], below,
        )

    def send_row_sums(step):
        k = top - step + (near * (2 * step - 1) if step < 2 else 0)
        row = row_of_traced(k)
        for h in (0, 1):
            row_sum(row, h).start()

    @pl.loop(0, 2 * n_rows)
    def _(i):
        @pl.when(jnp.logical_and(i == 1, near == 0))
        def _():
            column_arrival(0, 3)

        @pl.when(jnp.logical_and(i == 3, near == 0))
        def _():
            column_arrival(1, 3)

        @pl.when(i == 4)
        def _():
            row_arrival(0, 2)
            row_arrival(1, 2)

        @pl.when(i == 6 + near)
        def _():
            row_arrival(0, 3)
            row_arrival(1, 3)

        @pl.when(i == 2 * n_rows - 1)
        def _():
            finish(i - 1)
            send_row_sums(0)

            @pl.when(near == 0)
            def _():
                row_arrival(1, 1)

        compute(i)

        @pl.when(jnp.logical_and(i > 0, i < 2 * n_rows - 1))
        def _():
            finish(i - 1)

    finish(2 * n_rows - 1)
    for step in range(1, n_rows):
        send_row_sums(step)

    @pl.loop(0, 2 * n_rows)
    def _(i):
        row, h = row_of_traced(top - i // 2), i % 2
        mine = part.at[index(row, x, core), halves(h)]
        row_sum(row, h).wait_recv()
        add_into(mine, from_row.at[row, halves(h)])

        @pl.when(jnp.logical_and(row >= z, z > 0))
        def _():
            col_up(row, h).wait_recv()
            add_into(mine, from_below.at[row, halves(h)])

        @pl.when(jnp.logical_and(row <= z, z < top))
        def _():
            col_down(row, h).wait_recv()
            add_into(mine, from_above.at[row, halves(h)])

        @pl.when(row > z)
        def _():
            col_up(row, h).start()

        @pl.when(row < z)
        def _():
            col_down(row, h).start()

    out_ref[...] = part[me, :, pl.ds(0, width)]
    out_route[...] = part[me, :, pl.ds(width, LANES)]

    for c in weight_copies:
        c.wait_send()
    for k in range(n_rows):
        row = row_of(k)
        for p in (0, 1):
            if k == 0:

                @pl.when(z < top)
                def _(p=p):
                    up_copy(p, z).wait_send()

                @pl.when(z > 0)
                def _(p=p):
                    down_copy(p, z).wait_send()
            else:

                @pl.when(jnp.logical_and(row < z, z < top))
                def _(p=p, row=row):
                    up_copy(p, row).wait_send()

                @pl.when(jnp.logical_and(row > z, z > 0))
                def _(p=p, row=row):
                    down_copy(p, row).wait_send()

            row_forward(p, k, lambda p=p, row=row: row_copy(p, row).wait_send())
            sib_copy(p, row, x).wait_send()
            sib_copy(p, row, 1 - x).wait_send()

    @pl.when(jnp.logical_and(z > 0, z < top))
    def _():
        extra_copy(0, below).wait_send()
        extra_copy(1, above).wait_send()

    @pl.loop(0, 2 * n_rows)
    def _(i):
        to_sib(i).wait_send()
        row, h = i // 2, i % 2
        row_sum(row, h).wait_send()

        @pl.when(row != z)
        def _():
            col_up(row, h).wait_send()


def per_device_gather(tokens, grad_out, expert_ids, route_weight, w_gate, w_up, w_down):
    tok, width = tokens.shape
    n_expert = lax.axis_size("expert")
    n_rows = n_expert // 4
    hidden = w_gate.shape[2]
    chosen = expert_ids[:, :, None] == jnp.arange(LANES, dtype=jnp.int32)[None, None, :]
    dense = jnp.sum(jnp.where(chosen, route_weight[:, :, None].astype(jnp.float32), 0.0), axis=1)
    wide = width + LANES
    bf16, dma = jnp.bfloat16, pltpu.SemaphoreType.DMA
    vmem = pltpu.VMEM
    out, routes = pl.pallas_call(
        functools.partial(gather_kernel, n_rows),
        out_shape=(
            jax.ShapeDtypeStruct((tok, width), bf16),
            jax.ShapeDtypeStruct((tok, LANES), bf16),
        ),
        in_specs=[pl.BlockSpec(memory_space=pl.ANY)] * 6,
        out_specs=(pl.BlockSpec(memory_space=pltpu.VMEM), pl.BlockSpec(memory_space=pltpu.VMEM)),
        scratch_shapes=[
            vmem((n_expert, tok, width), bf16),
            vmem((n_expert, tok, wide), bf16),
            vmem((width, 2 * hidden), bf16),
            vmem((hidden, width), bf16),
            vmem((n_expert, tok, wide), bf16),
            vmem((n_expert // 2, tok, wide), bf16),
            vmem((n_rows, tok, wide), bf16),
            vmem((n_rows, tok, wide), bf16),
            vmem((n_rows, tok, wide), bf16),
            vmem((2 * tok, 2 * hidden), jnp.float32),
            vmem((2 * tok, hidden), jnp.float32),
            vmem((2 * tok, 2 * hidden), bf16),
            dma((3,)), dma((3,)), dma((3,)), dma((3,)),
            dma((2, n_expert)), dma((2, n_rows)), dma((2, n_rows)), dma((2, n_rows)),
            dma((2, n_expert // 2)), dma((2,)),
            dma((n_expert // 2,)), dma((n_expert // 2,)),
            dma((n_rows, 2)), dma((n_rows, 2)), dma((n_rows, 2)), dma((n_rows, 2)), dma((n_rows, 2)),
        ],
        compiler_params=pltpu.CompilerParams(
            collective_id=0, has_side_effects=True, vmem_limit_bytes=60 * 1024 * 1024
        ),
    )(tokens, grad_out, dense.astype(bf16), w_gate[0], w_up[0], w_down[0])
    grad_route = jnp.sum(
        jnp.where(chosen, routes[:, None, :].astype(jnp.float32), 0.0), axis=2
    ).astype(bf16)
    return (out, grad_route)


def per_device(*args):
    n_expert, top_k = lax.axis_size("expert"), args[2].shape[1]
    grid_fits = lax.axis_size("dp") == 2 and n_expert // 4 == 4 and n_expert % 4 == 0
    if grid_fits and 2 * top_k >= n_expert:
        return per_device_gather(*args)
    return per_device_exchange(*args)


def solution(mesh):
    return jax.shard_map(
        per_device,
        mesh=mesh,
        in_specs=(
            P(("dp", "expert"), None),
            P(("dp", "expert"), None),
            P(("dp", "expert"), None),
            P(("dp", "expert"), None),
            P("expert", "dp", None),
            P("expert", "dp", None),
            P("expert", None, "dp"),
        ),
        out_specs=(P(("dp", "expert"), None), P(("dp", "expert"), None)),
        check_vma=False,
    )
```
